256 devices in a mesh: section: 8 (over x, core), fsdp: 32 (over z, y).
Axes of the slice: x: 4, y: 4, z: 8, core: 2. Of those that a mesh axis runs over, the one named last changes fastest.
Arguments:
- activations: bfloat16 [8, 4096, 4096], P('section', 'fsdp'), may hold values from -6 to 6
- norm_gain: float32 [8, 4096], P('section'), may hold values from 0.1 to 1.9
- trunk_weight: bfloat16 [8, 4096, 4096], P('section', 'fsdp'), may hold values from -0.09375 to 0.09375
- head_weight: bfloat16 [4, 4096, 128], P(None, 'fsdp'), may hold values from -0.09375 to 0.09375
- head_mix: float32 [4, 128, 128], replicated, may hold values from -0.5 to 0.5
- head_steps: int32 [4], replicated, may hold values from 0 to 3, each once
- task_of: int32 [32, 1], replicated, may hold values from 0 to 3
- loss_ratio: float32 [4], replicated, may hold values from 0.5 to 2
- targets: bfloat16 [4096, 128], P('fsdp'), may hold values from -6 to 6
Outputs:
- passed: bfloat16 [8, 4096, 4096], P('section', 'fsdp')
- joined_grad: float32 [4096, 4096], P('fsdp', 'section')
- task_weights: float32 [4], replicated
- task_losses: float32 [4], replicated
The draws below stay inside these ranges and needn't reach their ends.
Inputs may be any that keep to these rules, and one draw needn't show every extreme that they name: `head_steps`: each value appears once. `task_of`: every task is named by at least one block.
All inputs are finite; a program needn't handle non-finite values.
Results may differ from the reference program's by a relative error of at most 0.017.
Values may be sent and summed in bfloat16 or wider, within the bound.
No kernel may reach another device: no remote copies, remote signals or barrier semaphores. Data moves between devices by JAX's collectives and lax.ppermute only.
A program may use at most 64 MiB of HBM per device.

```python
import math
import jax
import jax.numpy as jnp
from jax import lax

DW = 4096
TOK_DEV = 128
TASKS = 4
OUTS = 128
TOKENS = 4096
N_SECTION = 8
N_FSDP = 32


def block_scale(stream_key, dims, split, smallest, largest):
    def one(position, blocks):
        draws = jax.random.uniform(jax.random.fold_in(jax.random.fold_in(stream_key, 6), position), (blocks,), jnp.float32, smallest / len(split), largest / len(split))
        return jnp.repeat(jnp.exp(draws), dims[position] // blocks).reshape((-1,) + (1,) * (len(dims) - position - 1))

    factor_of = one(*split[0])
    for cut in split[1:]:
        factor_of = factor_of * one(*cut)
    return factor_of


def choose_distinct(key, rows, amount, top, lift):
    ranking = jax.random.permutation(jax.random.fold_in(key, 1), amount)
    boost = ranking
    for power in range(3):
        boost = boost * boost // amount
    boost = boost * lift // amount
    chance = jax.random.randint(jax.random.fold_in(key, 2), (rows, amount), 0, 4096) + boost
    holders = jax.random.permutation(jax.random.fold_in(key, 3), rows)[jnp.arange(amount) % rows]
    chance = jnp.where(jnp.arange(rows)[:, None] == holders[None, :], 1 << 14, chance)
    priority = chance * amount + jnp.arange(amount)
    return lax.top_k(priority.astype(jnp.int32), top)[1].astype(jnp.int32)


def bell_draw(key, shape, spread, limit, cuts=(), kind=jnp.bfloat16):
    factor_of = block_scale(key, shape, cuts, -0.22, 0.18) if cuts else 1.0
    entries = jax.random.normal(key, shape, jnp.float32) * spread * factor_of
    return jnp.minimum(jnp.maximum(entries, -limit), limit).astype(kind)


def setup_inputs(seed: int = 0) -> dict:
    keys = jax.random.split(jax.random.key(seed), 10)
    activations = bell_draw(keys[0], (N_SECTION, TOKENS, DW), 1.0, 6.0, ((0, 8), (1, 32)))
    norm_gain = jnp.clip(1.0 + 0.18 * jax.random.normal(keys[1], (N_SECTION, DW), jnp.float32), 0.1, 1.9)
    trunk_weight = bell_draw(keys[2], (N_SECTION, DW, DW), DW ** -0.5, 0.09375, ((0, 8), (1, 32)))
    head_weight = bell_draw(keys[3], (TASKS, DW, OUTS), DW ** -0.5, 0.09375, ((1, 32),))
    head_mix = bell_draw(keys[4], (TASKS, OUTS, OUTS), OUTS ** -0.5, 0.5, (), jnp.float32)
    head_steps = jax.random.permutation(keys[5], TASKS).astype(jnp.int32)
    task_of = choose_distinct(keys[6], N_FSDP, TASKS, 1, 2048)
    loss_ratio = jnp.clip(jnp.exp(jax.random.uniform(keys[7], (TASKS,), jnp.float32, math.log(0.5), math.log(2.0))), 0.5, 2.0)
    targets = bell_draw(keys[8], (TOKENS, OUTS), 1.0, 6.0, ((0, 32),))
    return dict(activations=activations, norm_gain=norm_gain, trunk_weight=trunk_weight, head_weight=head_weight, head_mix=head_mix, head_steps=head_steps, task_of=task_of, loss_ratio=loss_ratio, targets=targets)


EPS = 1e-05
ALPHA = 1.5

def rms_scale(values):
    return values * lax.rsqrt(lax.optimization_barrier(jnp.mean(values * values, axis=-1, keepdims=True)) + EPS)

def section_layer(hidden, gain, weight):
    normed = (rms_scale(hidden.astype(jnp.float32)) * gain).astype(jnp.bfloat16)
    pre = jnp.dot(normed, weight, preferred_element_type=jnp.float32).astype(jnp.bfloat16)
    output = (hidden.astype(jnp.float32) + jax.nn.silu(pre.astype(jnp.float32))).astype(jnp.bfloat16)
    return (normed, pre, output)

def head_loss(blocks, head_w, mix_w, step_total, target):
    head_in = rms_scale(blocks).astype(jnp.bfloat16)
    outputs = jnp.dot(head_in, head_w, preferred_element_type=jnp.float32)
    for depth_index in range(TASKS):
        active = (depth_index < step_total).astype(jnp.float32)
        outputs = outputs + active * jnp.tanh(jnp.dot(outputs, mix_w, precision=lax.Precision.HIGHEST))
    error_term = outputs - target.astype(jnp.float32)
    return 0.5 * jnp.sum(error_term * error_term)

def reference(activations, norm_gain, trunk_weight, head_weight, head_mix, head_steps, task_of, loss_ratio, targets):
    section_outs = lax.map(lambda section_args: section_layer(section_args[0], section_args[1], section_args[2])[2], (activations, norm_gain, trunk_weight))
    passed = jnp.concatenate([jnp.zeros((1, TOKENS, DW), jnp.bfloat16), section_outs[:-1]], axis=0)
    last_section = N_SECTION - 1
    normed_last, pre_last, out_last = section_layer(activations[last_section], norm_gain[last_section], trunk_weight[last_section])
    block_rows = out_last.astype(jnp.float32).reshape(N_FSDP, TOK_DEV, DW)
    task_ids = task_of[:, 0]
    target_blocks = targets.reshape(N_FSDP, TOK_DEV, OUTS)

    def per_block(block_args):
        blocks, task_id, target = block_args
        loss_value, pullback = jax.vjp(lambda inner: head_loss(inner, head_weight[task_id], head_mix[task_id], head_steps[task_id] + 1, target), blocks)
        return (loss_value, pullback(jnp.ones_like(loss_value))[0])
    block_losses, grad_out = lax.map(per_block, (block_rows, task_ids, target_blocks))
    onehot = (task_ids[:, None] == jnp.arange(TASKS)[None, :]).astype(jnp.float32)
    counts = TOK_DEV * lax.optimization_barrier(jnp.sum(onehot, axis=0))
    task_losses = lax.optimization_barrier(jnp.sum(onehot * block_losses[:, None], axis=0)) / (counts * OUTS)
    squares = lax.optimization_barrier(jnp.sum(grad_out * grad_out, axis=(1, 2)))
    grad_norms = jnp.sqrt(lax.optimization_barrier(jnp.sum(onehot * squares[:, None], axis=0)))
    target_norms = jnp.mean(grad_norms) * loss_ratio ** ALPHA
    ratios = target_norms / grad_norms
    task_weights = TASKS * ratios / jnp.sum(ratios)
    pre_float = pre_last.astype(jnp.float32)
    sigmoid_pre = jax.nn.sigmoid(pre_float)
    slope_term = sigmoid_pre * (1.0 + pre_float * (1.0 - sigmoid_pre))
    cotangent = (grad_out.reshape(TOKENS, DW) * slope_term).astype(jnp.bfloat16)
    row_weight = jnp.repeat(task_weights[task_ids], TOK_DEV)
    joined_grad = jnp.dot(normed_last.astype(jnp.float32).T, cotangent.astype(jnp.float32) * row_weight[:, None], precision=lax.Precision.HIGHEST)
    return (passed, joined_grad, task_weights, task_losses)
```

```python
import jax
import jax.numpy as jnp
from jax import lax
from jax.sharding import PartitionSpec as P

TASKS = 4
OUTS = 128
EPS = 1e-05
ALPHA = 1.5
NZ = 8
NY = 4
BOTH = ("section", "fsdp")
ALL = tuple(range(8))
F32 = jnp.float32
BF16 = jnp.bfloat16


def shift(x, dz, dy, sections=ALL):
    pairs = [
        (s * 32 + z * NY + y, s * 32 + (z + dz) % NZ * NY + (y + dy) % NY)
        for s in sections
        for z in range(NZ)
        for y in range(NY)
    ]
    return lax.ppermute(x, BOTH, pairs)


def flip(x, bit, sections=ALL):
    pairs = [(s * 32 + f, s * 32 + (f ^ bit)) for s in sections for f in range(32)]
    return lax.ppermute(x, BOTH, pairs)


def relay(x, links):
    return lax.ppermute(
        x, BOTH, [(a * 32 + f, b * 32 + f) for a, b in links for f in range(32)]
    )


def mm(a, b):
    return jnp.dot(a, b, preferred_element_type=F32)


def mm_high(a, b):
    return jnp.dot(a, b, precision=lax.Precision.HIGHEST)


def pick(stack, index):
    return lax.dynamic_index_in_dim(stack, index, 0, keepdims=False)


def cut(x, parts):
    rows, cols = x.shape
    return x.reshape(rows, parts, cols // parts).transpose(1, 0, 2)


def local(
    activations,
    norm_gain,
    trunk_weight,
    head_weight,
    head_mix,
    head_steps,
    task_of,
    loss_ratio,
    targets,
):
    section = lax.axis_index("section")
    member = lax.axis_index("fsdp")
    z = member // NY
    y = member % NY
    hidden = activations[0]
    rows, feats = hidden.shape
    tasks = task_of[:, 0]
    task = tasks[member]

    pieces = cut(trunk_weight[0], NY)
    slab = jnp.zeros((NY, rows, feats // NY), BF16)
    slab = lax.dynamic_update_index_in_dim(slab, pick(pieces, y), y, 0)
    for by in (1, 3, 2):
        got = shift(pick(pieces, (y + by) % NY), 0, by)
        slab = lax.dynamic_update_index_in_dim(slab, got, (y - by) % NY, 0)
    slab = slab.reshape(NY * rows, feats // NY)

    hidden_f = hidden.astype(F32)
    scale = lax.rsqrt(jnp.mean(hidden_f * hidden_f, axis=-1, keepdims=True) + EPS)
    normed = (hidden_f * scale * norm_gain[0]).astype(BF16)
    own = cut(normed, NZ)
    left = shift(own, 0, 1)
    right = shift(own, 0, -1)
    far = jnp.concatenate(
        [shift(left[: NZ // 2], 0, 1), shift(right[NZ // 2 :], 0, -1)], axis=0
    )
    tokens = jnp.concatenate([own, left, right, far], axis=1)

    half = slab.shape[0] // 2
    total = mm(pick(tokens, z), slab)
    up = down = slab
    for hop in range(1, NZ // 2):
        up = shift(up, 1, 0)
        down = shift(down, -1, 0)
        total = total + mm(pick(tokens, (z - hop) % NZ), up)
        total = total + mm(pick(tokens, (z + hop) % NZ), down)
    up = shift(up[:half], 1, 0)
    down = shift(down[half:], -1, 0)
    opposite = pick(tokens, (z + NZ // 2) % NZ)
    total = total + mm(opposite[:, :half], up) + mm(opposite[:, half:], down)

    parts = total.astype(BF16).reshape(NY, rows, feats // NY)
    pre = jnp.zeros((NY, rows, feats // NY), BF16)
    pre = lax.dynamic_update_index_in_dim(pre, parts[0], y, 0)
    for part, by in ((1, -1), (2, 1), (3, 2)):
        got = shift(parts[part], 0, by)
        pre = lax.dynamic_update_index_in_dim(pre, got, (y - by) % NY, 0)
    pre_f = pre.astype(F32)
    output = (cut(hidden_f, NY) + jax.nn.silu(pre_f)).astype(BF16)
    passed = relay(output, [(s, s + 1) for s in range(7)])
    passed = passed.transpose(1, 0, 2).reshape(1, rows, feats)

    mine = tokens.reshape(NZ, NY * rows, NY, rows)
    mine = jnp.where(
        y < 2,
        jnp.where(y == 0, mine[:, :, 0], mine[:, :, 1]),
        jnp.where(y == 2, mine[:, :, 2], mine[:, :, 3]),
    )
    pair = jnp.where(section == 7, mine, relay(mine, [(7, 6)]))
    near = relay(pair, [(7, 1), (6, 0)])
    first = jnp.where(section >= 6, pair, near)
    further = relay(first, [(7, 5), (6, 4), (1, 3), (0, 2)])
    normed_last = jnp.where((section == 0) | (section == 1) | (section >= 6), first, further)

    table = jnp.zeros((NY, TASKS, rows, OUTS), BF16)
    table = lax.dynamic_update_index_in_dim(table, head_weight, y, 0)
    for by in (1, 3, 2):
        got = shift(head_weight, 0, by, (0,))
        table = lax.dynamic_update_index_in_dim(table, got, (y - by) % NY, 0)
    weight = jnp.zeros((NZ, NY, rows, OUTS), BF16)

    def table_of(step):
        return lax.dynamic_index_in_dim(table, tasks[(z + step) % NZ * NY + y], 1, False)

    weight = lax.dynamic_update_index_in_dim(weight, table_of(0), z, 0)
    for step in (1, 7, 2, 6, 3, 5, 4):
        got = shift(table_of(step), step, 0, (0,))
        weight = lax.dynamic_update_index_in_dim(weight, got, (z - step) % NZ, 0)
    weight = relay(weight.reshape(NY, feats // NY, OUTS), [(0, 7)])

    h = output.astype(F32)
    h_scale = lax.rsqrt(jnp.sum(h * h, axis=(0, 2))[:, None] / feats + EPS)
    head_in = (h * h_scale).astype(BF16)
    zs = sum(mm(head_in[k], weight[k]) for k in range(NY))
    mix = pick(head_mix, task)
    steps = pick(head_steps, task)
    slopes = []
    for depth in range(TASKS):
        active = (depth <= steps).astype(F32)
        bend = jnp.tanh(mm_high(zs, mix))
        zs = zs + active * bend
        slopes.append(active * (1.0 - bend * bend))
    error = zs - targets.astype(F32)
    loss = 0.5 * jnp.sum(error * error)
    dz = error
    for slope in reversed(slopes):
        dz = dz + mm_high(slope * dz, mix.T)
    dz = dz.astype(BF16)
    g = jnp.stack([mm(dz, weight[k].T) for k in range(NY)]).astype(BF16).astype(F32)
    along = jnp.sum(g * h, axis=(0, 2))[:, None] / feats
    dh = h_scale * g - h * (h_scale * h_scale * h_scale * along)
    square = jnp.sum(dh * dh)
    sig = jax.nn.sigmoid(pre_f)
    cotangent = (dh * sig * (1.0 + pre_f * (1.0 - sig))).astype(BF16)

    scalars = jnp.zeros((8, 128), F32).at[0].set(square).at[1].set(loss)
    wide = feats // 8
    columns = [
        lax.slice_in_dim(cotangent[s // 2], s % 2 * wide, (s % 2 + 1) * wide, axis=1)
        for s in range(8)
    ]
    columns_own = columns[7]
    scalars_own = scalars
    for s in (0, 1, 4, 5, 2, 3, 6):
        got = relay(columns[s], [(7, s)])
        columns_own = jnp.where(section == s, got, columns_own)
        got = relay(scalars, [(7, s)])
        scalars_own = jnp.where(section == s, got, scalars_own)
    gathered = [columns_own]
    known = jnp.zeros((NZ, NY, 8, 128), F32)
    row = jnp.zeros((NY, 8, 128), F32)
    row = lax.dynamic_update_index_in_dim(row, scalars_own, y, 0)
    for by in (1, 3, 2):
        gathered.append(shift(columns_own, 0, by))
        got = shift(scalars_own, 0, by)
        row = lax.dynamic_update_index_in_dim(row, got, (y - by) % NY, 0)
    known = lax.dynamic_update_index_in_dim(known, row, z, 0)
    for bit in (4, 8, 16):
        known = known + flip(known, bit)
    squares = known[:, :, 0, 0].reshape(-1)
    losses = known[:, :, 1, 0].reshape(-1)

    onehot = (tasks[:, None] == jnp.arange(TASKS)[None, :]).astype(F32)
    counts = rows * jnp.sum(onehot, axis=0)
    task_losses = jnp.sum(onehot * losses[:, None], axis=0) / (counts * OUTS)
    grad_norms = jnp.sqrt(jnp.sum(onehot * squares[:, None], axis=0))
    ratios = jnp.mean(grad_norms) * loss_ratio**ALPHA / grad_norms
    task_weights = TASKS * ratios / jnp.sum(ratios)
    block_weights = jnp.sum(onehot * task_weights[None, :], axis=1).reshape(NZ, NY)
    row_weights = pick(block_weights, z)

    order = (y + jnp.array([0, -1, 1, 2])) % NY
    weighted = jnp.concatenate(
        [
            (block.astype(F32) * row_weights[order[k]]).astype(BF16)
            for k, block in enumerate(gathered)
        ],
        axis=0,
    )
    partial = lax.dot_general(
        normed_last, weighted, (((1,), (0,)), ((), ())), preferred_element_type=F32
    )
    joined = pick(partial, z)
    sent = partial.astype(BF16)
    for step in (4, 3, 5, 2, 6, 1, 7):
        joined = joined + shift(pick(sent, (z + step) % NZ), step, 0).astype(F32)
    return (passed, joined, task_weights, task_losses)


def solution(mesh):
    return jax.shard_map(
        local,
        mesh=mesh,
        in_specs=(
            P("section", "fsdp", None),
            P("section", None),
            P("section", "fsdp", None),
            P(None, "fsdp", None),
            P(),
            P(),
            P(),
            P(),
            P("fsdp", None),
        ),
        out_specs=(P("section", "fsdp", None), P("fsdp", "section"), P(), P()),
        check_vma=False,
    )
```

```python
import jax
import jax.numpy as jnp
from jax import lax
from jax.experimental import pallas as pl
from jax.experimental.pallas import tpu as pltpu
from jax.sharding import PartitionSpec as P

TASKS = 4
OUTS = 128
EPS = 1e-05
NZ = 8
NY = 4
ROWS = 128
FEATS = 4096
WIDE = FEATS // NY
SLAB = FEATS // NZ
COLS = FEATS // 8
HEAD = TASKS * ROWS // 8
BOTH = ("section", "fsdp")
ALL = tuple(range(8))
OFFSETS = (0, 1, -1, 2)
F32 = jnp.float32
BF16 = jnp.bfloat16
VMEM = pl.BlockSpec(memory_space=pltpu.VMEM)
SMEM = pl.BlockSpec(memory_space=pltpu.SMEM)


def shift(x, dz, dy, sections=ALL):
    pairs = [
        (s * 32 + z * NY + y, s * 32 + (z + dz) % NZ * NY + (y + dy) % NY)
        for s in sections
        for z in range(NZ)
        for y in range(NY)
    ]
    return lax.ppermute(x, BOTH, pairs)


def flip(x, bit, sections=ALL):
    pairs = [(s * 32 + f, s * 32 + (f ^ bit)) for s in sections for f in range(32)]
    return lax.ppermute(x, BOTH, pairs)


def relay(x, links):
    return lax.ppermute(
        x, BOTH, [(a * 32 + f, b * 32 + f) for a, b in links for f in range(32)]
    )


def mm(a, b):
    return jnp.dot(a, b, preferred_element_type=F32)


def mm_t(a, b, precision=None):
    return lax.dot_general(
        a, b, (((1,), (1,)), ((), ())), precision=precision, preferred_element_type=F32
    )


def shape(*dims, dtype=BF16):
    return jax.ShapeDtypeStruct(dims, dtype)


def kernel(body, outs, inputs, smem=(), scratch=()):
    return pl.pallas_call(
        body,
        out_shape=outs,
        in_specs=[SMEM if k in smem else VMEM for k in range(len(inputs))],
        out_specs=jax.tree.map(lambda _: VMEM, outs),
        scratch_shapes=scratch,
    )(*inputs)


def place():
    member = lax.axis_index("fsdp")
    return member // NY, member % NY


def split_body(weight, heads, block, *others):
    _, y = place()
    for by, out in zip(OFFSETS, (block,) + others):
        at = pl.multiple_of((y + by + NY) % NY * WIDE, WIDE)
        out[:ROWS] = weight[0, :, pl.ds(at, WIDE)]
    for k in range(8):
        block[ROWS:, k * OUTS : (k + 1) * OUTS] = heads[k // 2, k % 2 * HEAD : (k % 2 + 1) * HEAD]


def norm_body(hidden, gain, out):
    x = hidden[0].astype(F32)
    scale = lax.rsqrt(jnp.sum(x * x, axis=-1, keepdims=True) / FEATS + EPS)
    for k in range(NZ):
        part = slice(k * SLAB, (k + 1) * SLAB)
        out[k] = (x[:, part] * scale * gain[:, part]).astype(BF16)


def table_body(own, left, right, far, out):
    _, y = place()
    for by, blocks in zip(OFFSETS, (own, left, right, far)):
        at = (y - by + NY) % NY * ROWS
        for k in range(NZ):
            for half in range(2):
                start = pl.multiple_of(k * SLAB + at + half * HEAD, HEAD)
                out[pl.ds(start, HEAD)] = blocks[k, :, half * OUTS : (half + 1) * OUTS]


def product(where, tokens, terms, total=None, last=False):
    tile = WIDE // 2
    specs, inputs = [], []
    for at, pieces in terms:
        specs.append(
            pl.BlockSpec((1, NY * ROWS, SLAB), lambda n, w, at=at: (w[at], 0, 0))
        )
        inputs.append(tokens)
        for rhs, _, count in pieces:
            specs.append(pl.BlockSpec((count, tile), lambda n, w: (0, n)))
            inputs.append(rhs)
    if total is not None:
        specs.append(pl.BlockSpec((NY * ROWS, tile), lambda n, w: (0, n)))
        inputs.append(total)

    def body(_, *refs):
        refs = list(refs)
        outs = refs[len(inputs) :]
        value = None if total is None else refs[len(inputs) - 1][...]
        k = 0
        for _, pieces in terms:
            left = refs[k]
            k += 1
            for _, first, count in pieces:
                term = mm(left[0, :, first : first + count], refs[k][...])
                value = term if value is None else value + term
                k += 1
        if last:
            for at, out in enumerate(outs):
                out[...] = value[at * ROWS : (at + 1) * ROWS].astype(BF16)
        else:
            outs[0][...] = value

    if last:
        outs = [shape(ROWS, WIDE)] * NY
        out_specs = [pl.BlockSpec((ROWS, tile), lambda n, w: (0, n))] * NY
    else:
        outs = shape(NY * ROWS, WIDE, dtype=F32)
        out_specs = pl.BlockSpec((NY * ROWS, tile), lambda n, w: (0, n))
    return pl.pallas_call(
        body,
        out_shape=outs,
        grid_spec=pltpu.PrefetchScalarGridSpec(
            num_scalar_prefetch=1, grid=(2,), in_specs=specs, out_specs=out_specs
        ),
    )(where, *inputs)


def head_body(
    own, right, left, far, hidden, weight, mix, steps, tasks, targets, *refs
):
    output, pieces = refs[0], refs[1:9]
    pre, grads, scales = refs[9:]
    member = lax.axis_index("fsdp")
    _, y = place()
    task = tasks[member, 0]
    block = 32
    columns = [slice(s * COLS, (s + 1) * COLS) for s in range(8)]

    def forward(k, carry):
        lines = pl.ds(pl.multiple_of(k * block, block), block)
        sums = jnp.zeros((block, 1), F32)
        for by, part in zip((0, 1, -1, 2), (own, right, left, far)):
            at = pl.ds(pl.multiple_of((y + by + NY) % NY * WIDE, WIDE), WIDE)
            v = part[lines]
            pre[lines, at] = v
            v = v.astype(F32)
            h = (hidden[0, lines, at].astype(F32) + v * jax.nn.sigmoid(v)).astype(BF16)
            output[0, lines, at] = h
            h = h.astype(F32)
            sums = sums + jnp.sum(h * h, axis=1, keepdims=True)
        scales[lines] = jnp.broadcast_to(lax.rsqrt(sums / FEATS + EPS), (block, 128))
        return carry

    lax.fori_loop(0, ROWS // block, forward, 0)
    scale = scales[:, :1]
    z = jnp.zeros((ROWS, OUTS), F32)
    for column in columns:
        z = z + mm((output[0, :, column].astype(F32) * scale).astype(BF16), weight[column])
    mixed = mix[task]
    slopes = []
    for depth in range(TASKS):
        active = jnp.where(depth <= steps[task], 1.0, 0.0).astype(F32)
        bend = jnp.tanh(
            jnp.dot(z, mixed, precision=lax.Precision.HIGHEST, preferred_element_type=F32)
        )
        z = z + active * bend
        slopes.append(active * (1.0 - bend * bend))
    error = z - targets[...].astype(F32)
    loss = jnp.sum(jnp.sum(0.5 * error * error, axis=1, keepdims=True), axis=0, keepdims=True)
    dz = error
    for slope in reversed(slopes):
        dz = dz + mm_t(slope * dz, mixed, lax.Precision.HIGHEST)
    dz = dz.astype(BF16)
    along = jnp.zeros((ROWS, 1), F32)
    for column in columns:
        g = mm_t(dz, weight[column]).astype(BF16)
        grads[:, column] = g
        along = along + jnp.sum(
            g.astype(F32) * output[0, :, column].astype(F32), axis=1, keepdims=True
        )
    scales[:, 64:] = jnp.broadcast_to(along / FEATS, (ROWS, 64))

    def backward(k, square):
        lines = pl.ds(pl.multiple_of(k * block, block), block)
        one = scales[lines]
        r, c = one[:, :1], one[:, 64:65]
        c = r * r * r * c
        for s, column in enumerate(columns):
            dh = r * grads[lines, column].astype(F32) - c * output[0, lines, column].astype(F32)
            square = square + jnp.sum(dh * dh, axis=0, keepdims=True)
            p = pre[lines, column].astype(F32)
            sig = jax.nn.sigmoid(p)
            pieces[s][lines] = (dh * sig * (1.0 + p * (1.0 - sig))).astype(BF16)
        return square

    square = lax.fori_loop(0, ROWS // block, backward, jnp.zeros((1, COLS), F32))
    square = jnp.sum(square, axis=1, keepdims=True)
    line = lax.broadcasted_iota(jnp.int32, (8, COLS), 0)
    extra = jnp.zeros((8, COLS), F32)
    for at, value in ((0, square), (3, loss)):
        for k in range(3):
            piece = value.astype(BF16).astype(F32)
            extra = jnp.where(line == at + k, piece, extra)
            value = value - piece
    for piece in pieces:
        piece[ROWS:] = extra.astype(BF16)


def sums_body(own, left, right, far, tasks, out):
    z, y = place()
    line = lax.broadcasted_iota(jnp.int32, (8, 128), 0)
    sums = jnp.zeros((8, 128), F32)
    values = []
    for part in (own, left, right, far):
        v = part[ROWS:, :128].astype(F32)
        square = v[0:1] + v[1:2] + v[2:3]
        loss = v[3:4] + v[4:5] + v[5:6]
        values.append(jnp.where(line < TASKS, square, loss))
    for at in range(NY):
        value = jnp.zeros((8, 128), F32)
        for by, v in zip(OFFSETS, values):
            value = value + jnp.where((y - by + NY) % NY == at, v, 0.0)
        sums = sums + jnp.where(line % TASKS == tasks[z * NY + at, 0], value, 0.0)
    out[...] = sums


def joined_body(sums, ratio, own, left, right, far, normed, tasks, stats, kept, *sent):
    z, y = place()
    totals = sums[...]
    norms = jnp.sqrt(totals[:TASKS])
    rates = ratio[...]
    aims = jnp.sum(norms, axis=0, keepdims=True) / TASKS * (rates * jnp.sqrt(rates))
    ratios = aims / norms
    weights = TASKS * ratios / jnp.sum(ratios, axis=0, keepdims=True)
    line = lax.broadcasted_iota(jnp.int32, (TASKS, 128), 0)
    counts = jnp.zeros((TASKS, 128), F32)
    for k in range(NZ * NY):
        counts = counts + jnp.where(line == tasks[k, 0], float(ROWS), 0.0)
    stats[:TASKS] = weights
    stats[TASKS:] = totals[TASKS:] / (counts * OUTS)
    scaled = []
    for by, part in zip(OFFSETS, (own, left, right, far)):
        task = tasks[z * NY + (y - by + NY) % NY, 0]
        weight = jnp.sum(jnp.where(line == task, weights, 0.0), axis=0, keepdims=True)[:, :1]
        scaled.append((part[:ROWS].astype(F32) * weight).astype(BF16))
    scaled = jnp.concatenate(scaled, axis=0)
    kept[...] = mm(normed[z], scaled)
    for step, out in enumerate(sent):
        out[...] = mm(normed[(z + step + 1) % NZ], scaled).astype(BF16)


def local(
    activations,
    norm_gain,
    trunk_weight,
    head_weight,
    head_mix,
    head_steps,
    task_of,
    loss_ratio,
    targets,
):
    section = lax.axis_index("section")
    member = lax.axis_index("fsdp")
    z = member // NY
    y = member % NY
    tasks = task_of[:, 0]
    where = (z + jnp.arange(NZ, dtype=jnp.int32)) % NZ

    block, *others = kernel(
        split_body,
        [shape(ROWS + HEAD, WIDE)] + [shape(ROWS, WIDE)] * 3,
        (trunk_weight, head_weight),
    )
    others = [shift(other, 0, by) for other, by in zip(others, OFFSETS[1:])]

    own = kernel(norm_body, shape(NZ, ROWS, SLAB), (activations, norm_gain))
    others, own = lax.optimization_barrier((others, own))
    slab = jnp.concatenate(others, axis=0)
    left = shift(own, 0, 1)
    right = shift(own, 0, -1)
    far = jnp.concatenate(
        [shift(left[: NZ // 2], 0, 1), shift(right[NZ // 2 :], 0, -1)], axis=0
    )
    tokens = jnp.concatenate([own, left, right, far], axis=1)
    lanes = [tokens[:, :, k * ROWS : (k + 1) * ROWS] for k in range(NY)]

    def relative(blocks, by):
        at = (y + by) % NY
        return jnp.where(
            at < 2,
            jnp.where(at == 0, blocks[0], blocks[1]),
            jnp.where(at == 2, blocks[2], blocks[3]),
        )

    tokens = jnp.concatenate([relative(lanes, -by) for by in OFFSETS], axis=2)
    tokens = lax.optimization_barrier(tokens)

    mine = tokens[:, :, :ROWS].transpose(0, 2, 1)
    pair = relay(mine, [(7, 6)])

    up = down = block
    blocks = {0: block}
    for hop in range(1, NZ // 2):
        up = blocks[-hop] = shift(up, 1, 0)
        down = blocks[hop] = shift(down, -1, 0)
    heads_far = shift(up[ROWS:], 1, 0)
    block_far = shift(down[:ROWS], -1, 0)
    up = down = slab
    slabs = {0: slab}
    for hop in range(1, NZ // 2):
        up = slabs[-hop] = shift(up, 1, 0)
        down = slabs[hop] = shift(down, -1, 0)

    def terms(hops):
        return [(hop % NZ, [(blocks[hop], 0, ROWS), (slabs[hop], ROWS, SLAB - ROWS)]) for hop in hops]

    total = product(where, tokens, terms((0, -1, 1, -2, 2)))
    up, down, pair = lax.optimization_barrier((up, down, pair))
    pair = jnp.where(section == 7, mine, pair)
    next_to = relay(pair, [(7, 1), (6, 0)])
    up = shift(up[: 2 * ROWS], 1, 0)
    down = shift(down[2 * ROWS :], -1, 0)
    total = product(where, tokens, terms((-3, 3)), total)
    far_terms = [
        (NZ // 2, [(block_far, 0, ROWS), (up, ROWS, 2 * ROWS), (down, 3 * ROWS, ROWS)])
    ]
    parts = product(where, tokens, far_terms, total, True)
    parts, next_to = lax.optimization_barrier((parts, next_to))
    first = jnp.where(section >= 6, pair, next_to)
    further = relay(first, [(7, 5), (6, 4), (1, 3), (0, 2)])

    tables = jnp.zeros((NZ, HEAD, WIDE), BF16)
    for hop in range(1 - NZ // 2, NZ // 2 + 1):
        value = heads_far if hop == NZ // 2 else blocks[hop][ROWS:]
        tables = lax.dynamic_update_index_in_dim(tables, value, (z + hop) % NZ, 0)
    packed = 2 * OUTS
    by_task = [tables[:, :, t * packed : (t + 1) * packed] for t in range(TASKS)]

    def table_of(by):
        of = tasks[z * NY + (y + by) % NY]
        return jnp.where(
            of < 2,
            jnp.where(of == 0, by_task[0], by_task[1]),
            jnp.where(of == 2, by_task[2], by_task[3]),
        )

    table = [table_of(0)] + [shift(table_of(by), 0, by, (7,)) for by in OFFSETS[1:]]
    weight = kernel(table_body, shape(FEATS, OUTS), table)

    own_part = parts[0]
    from_right = shift(parts[1], 0, -1)
    from_left = shift(parts[2], 0, 1)
    from_far = shift(parts[3], 0, 2)
    output, *pieces = kernel(
        head_body,
        [shape(1, ROWS, FEATS)] + [shape(ROWS + 8, COLS)] * 8,
        (
            own_part,
            from_right,
            from_left,
            from_far,
            activations,
            weight,
            head_mix,
            head_steps,
            task_of,
            targets,
        ),
        smem=(7, 8),
        scratch=(
            pltpu.VMEM((ROWS, FEATS), BF16),
            pltpu.VMEM((ROWS, FEATS), BF16),
            pltpu.VMEM((ROWS, 128), F32),
        ),
    )
    passed = relay(output, [(s, s + 1) for s in range(7)])

    pieces, further = lax.optimization_barrier((pieces, further))
    normed_last = jnp.where((section < 2) | (section >= 6), first, further)
    piece = jnp.where(section == 7, pieces[7], jnp.zeros_like(pieces[7]))
    for s in (0, 1, 4, 5, 2, 3, 6):
        piece = piece + relay(pieces[s], [(7, s)])
    piece = lax.optimization_barrier(piece)
    gathered = [piece] + [shift(piece, 0, by) for by in OFFSETS[1:]]
    sums = kernel(sums_body, shape(8, 128, dtype=F32), (*gathered, task_of), smem=(4,))
    for bit in (4, 8, 16):
        sums = sums + flip(sums, bit)

    stats, joined, *sent = kernel(
        joined_body,
        [shape(8, 128, dtype=F32), shape(ROWS, COLS, dtype=F32)] + [shape(ROWS, COLS)] * 7,
        (sums, jnp.broadcast_to(loss_ratio[:, None], (TASKS, 128)), *gathered, normed_last, task_of),
        smem=(7,),
    )
    for step in (4, 3, 5, 2, 6, 1, 7):
        joined = joined + shift(sent[step - 1], step, 0).astype(F32)
    return (passed, joined, stats[:TASKS, 0], stats[TASKS:, 0])


def solution(mesh):
    return jax.shard_map(
        local,
        mesh=mesh,
        in_specs=(
            P("section", "fsdp", None),
            P("section", None),
            P("section", "fsdp", None),
            P(None, "fsdp", None),
            P(),
            P(),
            P(),
            P(),
            P("fsdp", None),
        ),
        out_specs=(P("section", "fsdp", None), P("fsdp", "section"), P(), P()),
        check_vma=False,
    )
```
